256 devices in a mesh: section: 32 (over z_lo, y, core), tensor: 8 (over z_hi, x).
Axes of the slice: x: 4, y: 4, z: 8 (z_hi: 2, z_lo: 4; z = z_hi * 4 + z_lo), core: 2. Of those that a mesh axis runs over, the one named last changes fastest.
Arguments:
- queries: bfloat16 [8192, 4096], P('section', 'tensor'), may hold values from -180 to 180
- memory: bfloat16 [512, 4096], P('section', 'tensor'), may hold values from -6 to 6
- key_weight: bfloat16 [65536, 4096], P('section', 'tensor'), may hold values from -0.09375 to 0.09375
- value_weight: bfloat16 [65536, 4096], P('section', 'tensor'), may hold values from -0.09375 to 0.09375
- grad_context: bfloat16 [8192, 4096], P('section', 'tensor'), may hold values from -6 to 6
- memory_lengths: int32 [4], replicated, may hold values from 64 to 128, as said below
Outputs:
- context: bfloat16 [8192, 4096], P('section', 'tensor')
- grad_queries: bfloat16 [8192, 4096], P('section', 'tensor')
- grad_memory: float32 [512, 4096], P('section', 'tensor')
The draws below stay inside these ranges and needn't reach their ends.
Inputs may be any that keep to these rules, and one draw needn't show every extreme that they name: `memory_lengths`: one reaction in every draw has all 128 encoder tokens.
All inputs are finite; a program needn't handle non-finite values.
Results may differ from the reference program's by a relative error of at most 0.0171.
The reference program's roundings to bfloat16 on the way count: a program that leaves them out, or rounds other values in their place, can miss the bound.
Values may be sent and summed in bfloat16 or wider, within the bound.
No kernel may reach another device: no remote copies, remote signals or barrier semaphores. Data moves between devices by JAX's collectives and lax.ppermute only.
A program may use at most 64 MiB of HBM per device.

```python
import jax
import jax.numpy as jnp
from jax import lax

D = 4096
HEADS = 64
HDIM = 64
REACT = 4
ENC_LEN = 128
DEC_LEN = 128
MEM_ROWS = 512
SECTION_ROWS = 8192
WEIGHT_ROWS = 65536


def draw_queries(key, part):
    base = jax.random.truncated_normal(key, -6.0, 6.0, (SECTION_ROWS, HEADS * HDIM), jnp.float32)
    return base.astype(jnp.bfloat16)


def draw_memory_lengths(key, part):
    shorter = jax.random.randint(jax.random.fold_in(key, 11), (REACT,), ENC_LEN // 2, ENC_LEN, jnp.int32)
    chosen = jax.random.randint(jax.random.fold_in(key, 13), (), 0, REACT, jnp.int32)
    position = jnp.arange(REACT, dtype=jnp.int32)
    return jnp.where(position == chosen, jnp.int32(ENC_LEN), shorter).astype(jnp.int32)


def block_scale(key, shape, cuts, smallest, high):
    level, own = 1.0, jax.random.fold_in(key, 6)
    for dim, shards_of in cuts:
        steps = jnp.exp(jax.random.uniform(jax.random.fold_in(own, dim), (shards_of,), jnp.float32, smallest / len(cuts), high / len(cuts)))
        level = level * jnp.repeat(steps, shape[dim] // shards_of).reshape([-1 if axis == dim else 1 for axis in range(len(shape))])
    return level


def normal_values(rng, shape, scale, reach, split=(), kind=jnp.bfloat16):
    entries = jax.random.normal(rng, shape, jnp.float32) * scale
    if len(split) > 0:
        entries = block_scale(rng, shape, split, -0.22, 0.18) * entries
    return jnp.clip(entries, min=-reach, max=reach).astype(kind)


def setup_inputs(seed: int = 0) -> dict:
    key_list = jax.random.split(jax.random.key(seed), 7)
    queries = draw_queries(jax.random.fold_in(key_list[6], 71), 0)
    memory = normal_values(key_list[1], (MEM_ROWS, D), 1.0, 6.0, ((0, 32), (1, 8)))
    key_weight = normal_values(key_list[2], (WEIGHT_ROWS, HEADS * HDIM), D ** -0.5, 0.09375, ((0, 32), (1, 8)))
    value_weight = normal_values(key_list[3], (WEIGHT_ROWS, HEADS * HDIM), D ** -0.5, 0.09375, ((0, 32), (1, 8)))
    grad_context = normal_values(key_list[4], (SECTION_ROWS, HEADS * HDIM), 1.0, 6.0, ((0, 32), (1, 8)))
    memory_lengths = draw_memory_lengths(jax.random.fold_in(key_list[6], 71), 0)
    return dict(queries=queries, memory=memory, key_weight=key_weight, value_weight=value_weight, grad_context=grad_context, memory_lengths=memory_lengths)


def one_layer(memory, lengths, query_rows, key_rows, value_rows, cot_rows):
    scale = HDIM ** -0.5
    keys = jnp.dot(memory, key_rows, preferred_element_type=jnp.float32).astype(jnp.bfloat16)
    values = jnp.dot(memory, value_rows, preferred_element_type=jnp.float32).astype(jnp.bfloat16)
    heads = keys.shape[1] // HDIM
    query_h = query_rows.reshape(REACT, DEC_LEN, heads, HDIM).astype(jnp.float32)
    key_h = keys.reshape(REACT, ENC_LEN, heads, HDIM).astype(jnp.float32)
    value_h = values.reshape(REACT, ENC_LEN, heads, HDIM).astype(jnp.float32)
    cot_h = cot_rows.reshape(REACT, DEC_LEN, heads, HDIM).astype(jnp.float32)
    scores = jnp.einsum("rqhd,rkhd->rhqk", query_h, key_h) * scale
    valid = jnp.arange(ENC_LEN, dtype=jnp.int32)[None, :] < lengths[:, None]
    scores = jnp.where(valid[:, None, None, :], scores, jnp.float32(-1e30))
    top = jnp.max(scores, axis=-1, keepdims=True)
    expo = jnp.exp(scores - top)
    probs = expo / jnp.sum(expo, axis=-1, keepdims=True)
    probs_b = probs.astype(jnp.bfloat16).astype(jnp.float32)
    context = jnp.einsum("rhqk,rkhd->rqhd", probs_b, value_h).astype(jnp.bfloat16)
    grad_p = jnp.einsum("rqhd,rkhd->rhqk", cot_h, value_h)
    delta = jnp.sum(probs * grad_p, axis=-1, keepdims=True)
    grad_s = (probs * (grad_p - delta) * scale).astype(jnp.bfloat16).astype(jnp.float32)
    grad_q = jnp.einsum("rhqk,rkhd->rqhd", grad_s, key_h).astype(jnp.bfloat16)
    grad_k = jnp.einsum("rhqk,rqhd->rkhd", grad_s, query_h).astype(jnp.bfloat16)
    grad_v = jnp.einsum("rhqk,rqhd->rkhd", probs_b, cot_h).astype(jnp.bfloat16)
    grad_k = grad_k.reshape(REACT * ENC_LEN, heads * HDIM)
    grad_v = grad_v.reshape(REACT * ENC_LEN, heads * HDIM)
    mem_grad = jnp.dot(grad_k, key_rows.T, preferred_element_type=jnp.float32)
    mem_grad = mem_grad + jnp.dot(grad_v, value_rows.T, preferred_element_type=jnp.float32)
    return (context.reshape(REACT * DEC_LEN, heads * HDIM), grad_q.reshape(REACT * DEC_LEN, heads * HDIM), mem_grad)


def reference(queries, memory, key_weight, value_weight, grad_context, memory_lengths):
    width = queries.shape[1]
    layer_count = key_weight.shape[0] // D
    stacked = (queries.reshape(layer_count, REACT * DEC_LEN, width),
               key_weight.reshape(layer_count, D, width),
               value_weight.reshape(layer_count, D, width),
               grad_context.reshape(layer_count, REACT * DEC_LEN, width))

    def step(total, items):
        context, grad_q, mem_grad = one_layer(memory, memory_lengths, items[0], items[1], items[2], items[3])
        return total + mem_grad, (context, grad_q)

    start = jnp.zeros((REACT * ENC_LEN, D), jnp.float32)
    total, outs = lax.scan(step, start, stacked)
    context = outs[0].reshape(layer_count * REACT * DEC_LEN, width)
    grad_q = outs[1].reshape(layer_count * REACT * DEC_LEN, width)
    return context, grad_q, total
```

```python
import jax
import jax.numpy as jnp
from jax import lax
from jax.experimental import pallas as pl
from jax.experimental.pallas import tpu as pltpu
from jax.sharding import Mesh, PartitionSpec as P

HDIM = 64
AXES = ("zl", "y", "core", "zh", "x")
NZ, NY, NC, NH, NX = 4, 4, 2, 2, 4
F32, BF16 = jnp.float32, jnp.bfloat16
VM = pl.BlockSpec(memory_space=pltpu.VMEM)
SM = pl.BlockSpec(memory_space=pltpu.SMEM)


def nt(a, b):
    return lax.dot_general(a, b, (((1,), (1,)), ((), ())), preferred_element_type=F32)


def nn(a, b):
    return lax.dot_general(a, b, (((1,), (0,)), ((), ())), preferred_element_type=F32)


def project_kernel(pair_ref, mem_ref, wk_ref, wv_ref, out_ref, rows_ref):
    base = pair_ref[0] * 64
    for x in range(NX):
        for i in range(2):
            start = pl.multiple_of(base + 32 * i, 32)
            part = mem_ref[:, x, pl.ds(start, 32), :].reshape(128, 512)
            rows_ref[128 * i : 128 * (i + 1), 512 * x : 512 * (x + 1)] = part
    out_ref[0] = nn(rows_ref[...], wk_ref[...])
    out_ref[1] = nn(rows_ref[...], wv_ref[...])


def project(pair, mem, wk, wv):
    return pl.pallas_call(
        project_kernel,
        out_shape=jax.ShapeDtypeStruct((2, 256, 512), F32),
        in_specs=[SM, VM, VM, VM],
        out_specs=VM,
        scratch_shapes=[pltpu.VMEM((256, 2048), BF16)],
        compiler_params=pltpu.CompilerParams(vmem_limit_bytes=20 << 20),
        cost_estimate=pl.CostEstimate(flops=2 * 2 * 256 * 2048 * 512, bytes_accessed=7 << 20, transcendentals=0),
        name="project",
    )(pair, mem, wk, wv)


def attend_kernel(pair_ref, len_ref, own_ref, got_ref, q_ref, g_ref, ctx_ref, gq_ref, gk_ref, gv_ref):
    scale = HDIM ** (-0.5)
    low = lax.broadcasted_iota(jnp.int32, (128, 128), 1) < HDIM
    token = lax.broadcasted_iota(jnp.int32, (2, 128, 128), 1)
    zero = jnp.zeros((128, 128), F32)

    def split(a):
        a = a.astype(F32)
        return jnp.concatenate([jnp.where(low, a, zero), jnp.where(low, zero, a)], axis=0).astype(BF16)

    for i in range(2):
        valid = token < len_ref[pair_ref[0] * 2 + i]
        for p in range(4):
            at = (slice(128 * i, 128 * (i + 1)), slice(128 * p, 128 * (p + 1)))
            ks = split((own_ref[0][at] + got_ref[0][at]).astype(BF16))
            vs = split((own_ref[1][at] + got_ref[1][at]).astype(BF16))
            q, g = q_ref[at], g_ref[at]
            qs, gs = split(q), split(g)
            s = nt(ks, q).reshape(2, 128, 128) * scale
            s = jnp.where(valid, s, F32(-1e30))
            e = jnp.exp(s - jnp.max(s, axis=1, keepdims=True))
            prob = e / jnp.sum(e, axis=1, keepdims=True)
            dp = nt(vs, g).reshape(2, 128, 128)
            delta = jnp.sum(prob * dp, axis=1, keepdims=True)
            ds = (prob * (dp - delta) * scale).astype(BF16)
            pb = prob.astype(BF16)
            ctx_ref[at] = nn(pb.reshape(256, 128).T, vs).astype(BF16)
            gq_ref[at] = nn(ds.reshape(256, 128).T, ks).astype(BF16)
            gk_ref[at] = nn(jnp.concatenate([ds[0], ds[1]], axis=1), qs).astype(BF16)
            gv_ref[at] = nn(jnp.concatenate([pb[0], pb[1]], axis=1), gs).astype(BF16)


def attend(pair, lengths, own, got, q, g):
    one = jax.ShapeDtypeStruct((256, 512), BF16)
    return pl.pallas_call(
        attend_kernel,
        out_shape=(one, one, one, one),
        in_specs=[SM, SM, VM, VM, VM, VM],
        out_specs=(VM, VM, VM, VM),
        compiler_params=pltpu.CompilerParams(vmem_limit_bytes=20 << 20),
        cost_estimate=pl.CostEstimate(flops=6 * 8 * 2 * 256 * 128 * 128, bytes_accessed=4 << 20, transcendentals=1 << 18),
        name="attend",
    )(pair, lengths, own, got, q, g)


def back_kernel(pair_ref, mine_ref, theirs_ref, wk_ref, wv_ref, out_ref):
    for side, ref in enumerate((mine_ref, theirs_ref)):
        pair = pair_ref[0] if side == 0 else 1 - pair_ref[0]
        for x in range(NX):
            at = slice(512 * x, 512 * (x + 1))
            r = (nt(ref[0], wk_ref[at]) + nt(ref[1], wv_ref[at])).astype(BF16)
            for i in range(2):
                start = pl.multiple_of(pair * 64 + 32 * i, 32)
                out_ref[:, x, pl.ds(start, 32), :] = r[128 * i : 128 * (i + 1)].reshape(NY, 32, 512)


def back(pair, mine, theirs, wk, wv):
    return pl.pallas_call(
        back_kernel,
        out_shape=jax.ShapeDtypeStruct((NY, NX, 128, 512), BF16),
        in_specs=[SM, VM, VM, VM, VM],
        out_specs=VM,
        compiler_params=pltpu.CompilerParams(vmem_limit_bytes=20 << 20),
        cost_estimate=pl.CostEstimate(flops=2 * 2 * 512 * 2048 * 512, bytes_accessed=7 << 20, transcendentals=0),
        name="back",
    )(pair, mine, theirs, wk, wv)


def swap_route(flip):
    return [(c * NH + h, h * NH + (c ^ flip)) for c in range(NC) for h in range(NH)]


def gather(memory):
    high = lax.axis_index("zh")
    near = lax.ppermute(memory, ("core", "zh"), swap_route(0))
    far = lax.ppermute(memory, ("core", "zh"), swap_route(1))
    first = high == 0
    both = jnp.concatenate([jnp.where(first, near, far), jnp.where(first, far, near)], axis=0)
    column = lax.all_to_all(jnp.broadcast_to(both, (NZ, 32, 512)), "zl", 0, 0)
    column = column.reshape(128, 512)
    return lax.all_to_all(jnp.broadcast_to(column, (NY * NX, 128, 512)), ("y", "x"), 0, 0)


def scatter(parts):
    high = lax.axis_index("zh")
    got = lax.all_to_all(parts, ("y", "x"), 0, 0)
    plane = jnp.sum(got.astype(F32), axis=0).astype(BF16).reshape(NZ, 32, 512)
    line = jnp.sum(lax.all_to_all(plane, "zl", 0, 0).astype(F32), axis=0)
    first = high == 0
    near = lax.ppermute(jnp.where(first, line[:16], line[16:]), ("core", "zh"), send_route(0))
    far = lax.ppermute(jnp.where(first, line[16:], line[:16]), ("core", "zh"), send_route(1))
    return near + far


def send_route(flip):
    return [(c * NH + h, (h ^ flip) * NH + c) for c in range(NC) for h in range(NH)]


def body(queries, memory, key_weight, value_weight, grad_context, memory_lengths):
    pair = lax.axis_index("core").astype(jnp.int32).reshape(1)
    mem = gather(memory).reshape(NY, NX, 128, 512)
    other = project(1 - pair, mem, key_weight, value_weight)
    got = lax.ppermute(other, "core", [(0, 1), (1, 0)])
    own = project(pair, mem, key_weight, value_weight)
    ctx, gq, gk, gv = attend(pair, memory_lengths, own, got, queries, grad_context)
    mine = jnp.stack([gk, gv])
    theirs = lax.ppermute(mine, "core", [(0, 1), (1, 0)])
    parts = back(pair, mine, theirs, key_weight, value_weight)
    return ctx, gq, scatter(parts.reshape(NY * NX, 128, 512))


def solution(mesh):
    fine = Mesh(mesh.devices.reshape(NZ, NY, NC, NH, NX), AXES)
    spec = P(("zl", "y", "core"), ("zh", "x"))
    return jax.shard_map(
        body,
        mesh=fine,
        in_specs=(spec, spec, spec, spec, spec, P()),
        out_specs=(spec, spec, spec),
        check_vma=False,
    )
```

```python
import functools

import jax
import jax.numpy as jnp
from jax import lax
from jax.experimental import pallas as pl
from jax.experimental.pallas import tpu as pltpu
from jax.sharding import Mesh, PartitionSpec as P

HDIM = 64
AXES = ("zl", "y", "core", "zh", "x")
NZ, NY, NC, NH, NX = 4, 4, 2, 2, 4
F32, BF16 = jnp.float32, jnp.bfloat16
VM = pl.BlockSpec(memory_space=pltpu.VMEM)
SM = pl.BlockSpec(memory_space=pltpu.SMEM)


def nt(a, b):
    return lax.dot_general(a, b, (((1,), (1,)), ((), ())), preferred_element_type=F32)


def nn(a, b):
    return lax.dot_general(a, b, (((1,), (0,)), ((), ())), preferred_element_type=F32)


def project_kernel(other, core_ref, mem_ref, wk_ref, wv_ref, out_ref, rows_ref):
    base = (1 - core_ref[0] if other else core_ref[0]) * 64
    for x in range(NX):
        for i in range(2):
            start = pl.multiple_of(base + 32 * i, 32)
            part = mem_ref[:, x, pl.ds(start, 32), :].reshape(128, 512)
            rows_ref[128 * i : 128 * (i + 1), 512 * x : 512 * (x + 1)] = part
    out_ref[0] = nn(rows_ref[...], wk_ref[...])
    out_ref[1] = nn(rows_ref[...], wv_ref[...])


def project(other, core, mem, wk, wv):
    return pl.pallas_call(
        functools.partial(project_kernel, other),
        out_shape=jax.ShapeDtypeStruct((2, 256, 512), F32),
        in_specs=[SM, VM, VM, VM],
        out_specs=VM,
        scratch_shapes=[pltpu.VMEM((256, 2048), BF16)],
        compiler_params=pltpu.CompilerParams(vmem_limit_bytes=20 << 20),
        cost_estimate=pl.CostEstimate(flops=2 * 2 * 256 * 2048 * 512, bytes_accessed=7 << 20, transcendentals=0),
        name="project",
    )(core, mem, wk, wv)


def attend_kernel(pair_ref, len_ref, own_ref, got_ref, q_ref, g_ref, ctx_ref, gq_ref, grad_ref):
    scale = HDIM ** (-0.5)
    low = lax.broadcasted_iota(jnp.int32, (128, 128), 1) < HDIM
    token = lax.broadcasted_iota(jnp.int32, (2, 128, 128), 1)
    zero = jnp.zeros((128, 128), F32)

    def split(a):
        a = a.astype(F32)
        return jnp.concatenate([jnp.where(low, a, zero), jnp.where(low, zero, a)], axis=0).astype(BF16)

    for i in range(2):
        valid = token < len_ref[pair_ref[0] * 2 + i]
        for p in range(4):
            at = (slice(128 * i, 128 * (i + 1)), slice(128 * p, 128 * (p + 1)))
            ks = split((own_ref[0][at] + got_ref[0][at]).astype(BF16))
            vs = split((own_ref[1][at] + got_ref[1][at]).astype(BF16))
            q, g = q_ref[at], g_ref[at]
            qs, gs = split(q), split(g)
            s = nt(ks, q).reshape(2, 128, 128) * scale
            s = jnp.where(valid, s, F32(-1e30))
            e = jnp.exp(s - jnp.max(s, axis=1, keepdims=True))
            prob = e / jnp.sum(e, axis=1, keepdims=True)
            dp = nt(vs, g).reshape(2, 128, 128)
            delta = jnp.sum(prob * dp, axis=1, keepdims=True)
            ds = (prob * (dp - delta) * scale).astype(BF16)
            pb = prob.astype(BF16)
            ctx_ref[at] = nn(pb.reshape(256, 128).T, vs).astype(BF16)
            gq_ref[at] = nn(ds.reshape(256, 128).T, ks).astype(BF16)
            grad_ref[(0, *at)] = nn(jnp.concatenate([ds[0], ds[1]], axis=1), qs).astype(BF16)
            grad_ref[(1, *at)] = nn(jnp.concatenate([pb[0], pb[1]], axis=1), gs).astype(BF16)


def attend(pair, lengths, own, got, q, g):
    one = jax.ShapeDtypeStruct((256, 512), BF16)
    return pl.pallas_call(
        attend_kernel,
        out_shape=(one, one, jax.ShapeDtypeStruct((2, 256, 512), BF16)),
        in_specs=[SM, SM, VM, VM, VM, VM],
        out_specs=(VM, VM, VM),
        compiler_params=pltpu.CompilerParams(vmem_limit_bytes=20 << 20),
        cost_estimate=pl.CostEstimate(flops=6 * 8 * 2 * 256 * 128 * 128, bytes_accessed=4 << 20, transcendentals=1 << 18),
        name="attend",
    )(pair, lengths, own, got, q, g)


def back_kernel(pair_ref, mine_ref, theirs_ref, wk_ref, wv_ref, out_ref):
    for side, ref in enumerate((mine_ref, theirs_ref)):
        pair = pair_ref[0] if side == 0 else 1 - pair_ref[0]
        for x in range(NX):
            at = slice(512 * x, 512 * (x + 1))
            r = (nt(ref[0], wk_ref[at]) + nt(ref[1], wv_ref[at])).astype(BF16)
            for i in range(2):
                start = pl.multiple_of(pair * 64 + 32 * i, 32)
                out_ref[:, x, pl.ds(start, 32), :] = r[128 * i : 128 * (i + 1)].reshape(NY, 32, 512)


def back(pair, mine, theirs, wk, wv):
    return pl.pallas_call(
        back_kernel,
        out_shape=jax.ShapeDtypeStruct((NY, NX, 128, 512), BF16),
        in_specs=[SM, VM, VM, VM, VM],
        out_specs=VM,
        compiler_params=pltpu.CompilerParams(vmem_limit_bytes=20 << 20),
        cost_estimate=pl.CostEstimate(flops=2 * 2 * 512 * 2048 * 512, bytes_accessed=7 << 20, transcendentals=0),
        name="back",
    )(pair, mine, theirs, wk, wv)


def swap(block):
    return lax.ppermute(block, "core", [(0, 1), (1, 0)])


def fan_kernel(core_ref, ring_ref, got_ref, out_ref):
    core = core_ref[0]
    for z in range(NZ):
        for c in range(NC):
            here = (core == c).astype(jnp.int32)
            block = jnp.where(here == 1, ring_ref[z, core].astype(F32), got_ref[z].astype(F32)).astype(BF16)
            for k in range(NY * NX):
                out_ref[k, 32 * z + 16 * c : 32 * z + 16 * (c + 1), :] = block


def fan(core, ring, got):
    return pl.pallas_call(
        fan_kernel,
        out_shape=jax.ShapeDtypeStruct((NY * NX, 128, 512), BF16),
        in_specs=[SM, VM, VM],
        out_specs=VM,
        compiler_params=pltpu.CompilerParams(vmem_limit_bytes=12 << 20),
        cost_estimate=pl.CostEstimate(flops=1 << 20, bytes_accessed=3 << 20, transcendentals=0),
        name="fan",
    )(core, ring, got)


def spread_kernel(core_ref, block_ref, out_ref):
    block = block_ref[...]
    for k in range(NZ * NH):
        out_ref[k] = block


def pick_kernel(core_ref, ring_ref, out_ref):
    for z in range(NZ):
        out_ref[z] = ring_ref[z, 1 - core_ref[0]]


def join_kernel(core_ref, keep_ref, got_ref, out_ref):
    for z in range(NZ):
        out_ref[z, core_ref[0]] = keep_ref[z]
        out_ref[z, 1 - core_ref[0]] = got_ref[z]


def small(kernel, name, shape, *args):
    return pl.pallas_call(
        kernel,
        out_shape=jax.ShapeDtypeStruct(shape, BF16),
        in_specs=[SM] + [VM] * (len(args) - 1),
        out_specs=VM,
        compiler_params=pltpu.CompilerParams(vmem_limit_bytes=4 << 20),
        cost_estimate=pl.CostEstimate(flops=0, bytes_accessed=1 << 18, transcendentals=0),
        name=name,
    )(*args)


def gather(memory, core):
    copies = small(spread_kernel, "spread", (NZ * NH, 16, 512), core, memory)
    ring = lax.all_to_all(copies, ("zl", "zh"), 0, 0).reshape(NZ, NH, 16, 512)
    got = swap(small(pick_kernel, "pick", (NZ, 16, 512), core, ring))
    return lax.all_to_all(fan(core, ring, got), ("y", "x"), 0, 0)


def fold_kernel(core_ref, parts_ref, keep_ref, send_ref):
    core = core_ref[0]
    for side, ref in enumerate((keep_ref, send_ref)):
        half = core if side == 0 else 1 - core
        for z in range(NZ):
            start = pl.multiple_of(32 * z + 16 * half, 16)
            ref[z] = jnp.sum(parts_ref[:, pl.ds(start, 16), :].astype(F32), axis=0).astype(BF16)


def fold(core, parts):
    half = jax.ShapeDtypeStruct((NZ, 16, 512), BF16)
    return pl.pallas_call(
        fold_kernel,
        out_shape=(half, half),
        in_specs=[SM, VM],
        out_specs=(VM, VM),
        compiler_params=pltpu.CompilerParams(vmem_limit_bytes=12 << 20),
        cost_estimate=pl.CostEstimate(flops=1 << 20, bytes_accessed=3 << 20, transcendentals=0),
        name="fold",
    )(core, parts)


def scatter(parts, core):
    keep, send = fold(core, lax.all_to_all(parts, ("y", "x"), 0, 0))
    ring = small(join_kernel, "join", (NZ, NH, 16, 512), core, keep, swap(send))
    ring = lax.all_to_all(ring.reshape(NZ * NH, 16, 512), ("zl", "zh"), 0, 0)
    return jnp.sum(ring.astype(F32), axis=0)


def body(queries, memory, key_weight, value_weight, grad_context, memory_lengths):
    core = lax.axis_index("core").astype(jnp.int32).reshape(1)
    mem = gather(memory, core).reshape(NY, NX, 128, 512)
    other = project(True, core, mem, key_weight, value_weight)
    got = swap(other)
    own = project(False, core, mem, key_weight, value_weight)
    ctx, gq, mine = attend(core, memory_lengths, own, got, queries, grad_context)
    parts = back(core, mine, swap(mine), key_weight, value_weight)
    return ctx, gq, scatter(parts.reshape(NY * NX, 128, 512), core)


def solution(mesh):
    fine = Mesh(mesh.devices.reshape(NZ, NY, NC, NH, NX), AXES)
    spec = P(("zl", "y", "core"), ("zh", "x"))
    return jax.shard_map(
        body,
        mesh=fine,
        in_specs=(spec, spec, spec, spec, spec, P()),
        out_specs=(spec, spec, spec),
        check_vma=False,
    )
```

```python
import functools

import jax
import jax.numpy as jnp
from jax import lax
from jax.experimental import pallas as pl
from jax.experimental.pallas import tpu as pltpu
from jax.sharding import Mesh, PartitionSpec as P

HDIM = 64
AXES = ("zl", "y", "core", "zh", "x")
NZ, NY, NC, NH, NX = 4, 4, 2, 2, 4
F32, BF16 = jnp.float32, jnp.bfloat16
VM = pl.BlockSpec(memory_space=pltpu.VMEM)
SM = pl.BlockSpec(memory_space=pltpu.SMEM)


def nt(a, b):
    return lax.dot_general(a, b, (((1,), (1,)), ((), ())), preferred_element_type=F32)


def nn(a, b):
    return lax.dot_general(a, b, (((1,), (0,)), ((), ())), preferred_element_type=F32)


def place(core, y, x, far, near):
    return jnp.where(core == 0, y + far, y + near) % NY, jnp.where(core == 0, x + near, x + far) % NX


def project_kernel(other, core_ref, y_ref, x_ref, b0_ref, b1_ref, b2_ref, b3_ref, wk_ref, wv_ref, out_ref, rows_ref):
    base = (1 - core_ref[0] if other else core_ref[0]) * 64
    for far, ref in enumerate((b0_ref, b1_ref, b2_ref, b3_ref)):
        for near in range(4):
            y, x = place(core_ref[0], y_ref[0], x_ref[0], 4 - far, 4 - near)
            for i in range(2):
                start = pl.multiple_of(base + 32 * i, 32)
                row = pl.multiple_of(128 * i + 32 * y, 32)
                rows_ref[x, pl.ds(row, 32), :] = ref[near, pl.ds(start, 32), :]
    rows = jnp.concatenate([rows_ref[x] for x in range(NX)], axis=1)
    out_ref[0] = nn(rows, wk_ref[...])
    out_ref[1] = nn(rows, wv_ref[...])


def project(other, here, blocks, wk, wv):
    return pl.pallas_call(
        functools.partial(project_kernel, other),
        out_shape=jax.ShapeDtypeStruct((2, 256, 512), F32),
        in_specs=[SM] * 3 + [VM] * 6,
        out_specs=VM,
        scratch_shapes=[pltpu.VMEM((NX, 256, 512), BF16)],
        compiler_params=pltpu.CompilerParams(vmem_limit_bytes=20 << 20),
        cost_estimate=pl.CostEstimate(flops=2 * 2 * 256 * 2048 * 512, bytes_accessed=7 << 20, transcendentals=0),
        name="project",
    )(*here, *blocks, wk, wv)


def attend_kernel(pair_ref, len_ref, own_ref, got_ref, q_ref, g_ref, ctx_ref, gq_ref, grad_ref):
    scale = HDIM ** (-0.5)
    low = lax.broadcasted_iota(jnp.int32, (128, 128), 1) < HDIM
    token = lax.broadcasted_iota(jnp.int32, (2, 128, 128), 1)
    zero = jnp.zeros((128, 128), F32)

    def split(a):
        a = a.astype(F32)
        return jnp.concatenate([jnp.where(low, a, zero), jnp.where(low, zero, a)], axis=0).astype(BF16)

    for i in range(2):
        valid = token < len_ref[pair_ref[0] * 2 + i]
        for p in range(4):
            at = (slice(128 * i, 128 * (i + 1)), slice(128 * p, 128 * (p + 1)))
            ks = split((own_ref[0][at] + got_ref[0][at]).astype(BF16))
            vs = split((own_ref[1][at] + got_ref[1][at]).astype(BF16))
            q, g = q_ref[at], g_ref[at]
            qs, gs = split(q), split(g)
            s = nt(ks, q).reshape(2, 128, 128) * scale
            s = jnp.where(valid, s, F32(-1e30))
            e = jnp.exp(s - jnp.max(s, axis=1, keepdims=True))
            prob = e / jnp.sum(e, axis=1, keepdims=True)
            dp = nt(vs, g).reshape(2, 128, 128)
            delta = jnp.sum(prob * dp, axis=1, keepdims=True)
            ds = (prob * (dp - delta) * scale).astype(BF16)
            pb = prob.astype(BF16)
            ctx_ref[at] = nn(pb.reshape(256, 128).T, vs).astype(BF16)
            gq_ref[at] = nn(ds.reshape(256, 128).T, ks).astype(BF16)
            grad_ref[(0, *at)] = nn(jnp.concatenate([ds[0], ds[1]], axis=1), qs).astype(BF16)
            grad_ref[(1, *at)] = nn(jnp.concatenate([pb[0], pb[1]], axis=1), gs).astype(BF16)


def attend(pair, lengths, own, got, q, g):
    one = jax.ShapeDtypeStruct((256, 512), BF16)
    return pl.pallas_call(
        attend_kernel,
        out_shape=(one, one, jax.ShapeDtypeStruct((2, 256, 512), BF16)),
        in_specs=[SM, SM, VM, VM, VM, VM],
        out_specs=(VM, VM, VM),
        compiler_params=pltpu.CompilerParams(vmem_limit_bytes=20 << 20),
        cost_estimate=pl.CostEstimate(flops=6 * 8 * 2 * 256 * 128 * 128, bytes_accessed=4 << 20, transcendentals=1 << 18),
        name="attend",
    )(pair, lengths, own, got, q, g)


def stage_kernel(wk_ref, wv_ref, after_ref, k_ref, v_ref, sems):
    copies = [
        pltpu.make_async_copy(wk_ref, k_ref, sems.at[0]),
        pltpu.make_async_copy(wv_ref, v_ref, sems.at[1]),
    ]
    for copy in copies:
        copy.start()
    for copy in copies:
        copy.wait()


def stage(wk, wv, after):
    leave = pl.BlockSpec(memory_space=pl.ANY)
    return pl.pallas_call(
        stage_kernel,
        out_shape=(jax.ShapeDtypeStruct(wk.shape, BF16), jax.ShapeDtypeStruct(wv.shape, BF16)),
        in_specs=[leave, leave, leave],
        out_specs=(VM, VM),
        scratch_shapes=[pltpu.SemaphoreType.DMA((2,))],
        compiler_params=pltpu.CompilerParams(vmem_limit_bytes=10 << 20),
        cost_estimate=pl.CostEstimate(flops=0, bytes_accessed=8 << 20, transcendentals=0),
        name="stage",
    )(wk, wv, after)


def back_kernel(core_ref, y_ref, x_ref, mine_ref, theirs_ref, wk_ref, wv_ref, o0_ref, o1_ref, o2_ref, o3_ref, all_ref):
    for side, ref in enumerate((mine_ref, theirs_ref)):
        pair = core_ref[0] if side == 0 else 1 - core_ref[0]
        for x in range(NX):
            at = slice(512 * x, 512 * (x + 1))
            r = (nt(ref[0], wk_ref[at]) + nt(ref[1], wv_ref[at])).astype(BF16)
            for i in range(2):
                start = pl.multiple_of(pair * 64 + 32 * i, 32)
                all_ref[:, x, pl.ds(start, 32), :] = r[128 * i : 128 * (i + 1)].reshape(NY, 32, 512)
    for far, ref in enumerate((o0_ref, o1_ref, o2_ref, o3_ref)):
        for near in range(4):
            y, x = place(core_ref[0], y_ref[0], x_ref[0], far, near)
            ref[near] = all_ref[y, x]


def back(here, mine, theirs, wk, wv):
    part = jax.ShapeDtypeStruct((4, 128, 512), BF16)
    return pl.pallas_call(
        back_kernel,
        out_shape=(part, part, part, part),
        in_specs=[SM] * 3 + [VM] * 4,
        out_specs=(VM, VM, VM, VM),
        scratch_shapes=[pltpu.VMEM((NY, NX, 128, 512), BF16)],
        compiler_params=pltpu.CompilerParams(vmem_limit_bytes=20 << 20),
        cost_estimate=pl.CostEstimate(flops=2 * 2 * 512 * 2048 * 512, bytes_accessed=7 << 20, transcendentals=0),
        name="back",
    )(*here, mine, theirs, wk, wv)


def swap(block):
    return lax.ppermute(block, "core", [(0, 1), (1, 0)])


def route(along, shift):
    pairs = []
    for y in range(NY):
        for c in range(NC):
            for x in range(NX):
                to = (y, (x + shift) % NX) if c == along else ((y + shift) % NY, x)
                pairs.append(((y * NC + c) * NX + x, (to[0] * NC + c) * NX + to[1]))
    return pairs


def shifted(along, blocks):
    return [lax.ppermute(b, ("y", "core", "x"), route(along, k)) for k, b in zip((1, 2, 3), blocks)]


def column_kernel(core_ref, ring_ref, got_ref, out_ref):
    core = core_ref[0]
    for z in range(NZ):
        own = pl.multiple_of(32 * z + 16 * core, 16)
        out_ref[pl.ds(own, 16), :] = ring_ref[z, core]
        other = pl.multiple_of(32 * z + 16 * (1 - core), 16)
        out_ref[pl.ds(other, 16), :] = got_ref[z]


def pack_kernel(core_ref, *refs):
    for k in range(4):
        refs[4][k] = refs[k][...]


def spread_kernel(core_ref, block_ref, out_ref):
    block = block_ref[...]
    for k in range(NZ * NH):
        out_ref[k] = block


def pick_kernel(core_ref, ring_ref, out_ref):
    for z in range(NZ):
        out_ref[z] = ring_ref[z, 1 - core_ref[0]]


def join_kernel(core_ref, keep_ref, got_ref, out_ref):
    for z in range(NZ):
        out_ref[z, core_ref[0]] = keep_ref[z]
        out_ref[z, 1 - core_ref[0]] = got_ref[z]


def small(kernel, name, shape, *args):
    return pl.pallas_call(
        kernel,
        out_shape=jax.ShapeDtypeStruct(shape, BF16),
        in_specs=[SM] + [VM] * (len(args) - 1),
        out_specs=VM,
        compiler_params=pltpu.CompilerParams(vmem_limit_bytes=4 << 20),
        cost_estimate=pl.CostEstimate(flops=0, bytes_accessed=1 << 18, transcendentals=0),
        name=name,
    )(*args)


def gather(memory, core):
    copies = small(spread_kernel, "spread", (NZ * NH, 16, 512), core, memory)
    ring = lax.all_to_all(copies, ("zl", "zh"), 0, 0).reshape(NZ, NH, 16, 512)
    got = swap(small(pick_kernel, "pick", (NZ, 16, 512), core, ring))
    column = small(column_kernel, "column", (128, 512), core, ring, got)
    blocks = small(pack_kernel, "pack", (4, 128, 512), core, column, *shifted(0, [column] * 3))
    return [blocks, *shifted(1, [blocks] * 3)]


def total_kernel(p0_ref, p1_ref, p2_ref, p3_ref, *out_refs):
    for near, ref in enumerate(out_refs):
        total = p0_ref[near].astype(F32) + p1_ref[near].astype(F32)
        ref[...] = (total + p2_ref[near].astype(F32) + p3_ref[near].astype(F32)).astype(BF16)


def total(parts):
    one = jax.ShapeDtypeStruct((128, 512), BF16)
    return pl.pallas_call(
        total_kernel,
        out_shape=(one, one, one, one),
        in_specs=[VM] * 4,
        out_specs=(VM,) * 4,
        compiler_params=pltpu.CompilerParams(vmem_limit_bytes=8 << 20),
        cost_estimate=pl.CostEstimate(flops=1 << 20, bytes_accessed=5 << 19, transcendentals=0),
        name="total",
    )(*parts)


def fold_kernel(core_ref, p0_ref, p1_ref, p2_ref, p3_ref, keep_ref, send_ref):
    core = core_ref[0]
    for side, out in enumerate((keep_ref, send_ref)):
        half = core if side == 0 else 1 - core
        for z in range(NZ):
            at = pl.ds(pl.multiple_of(32 * z + 16 * half, 16), 16)
            total = p0_ref[at, :].astype(F32) + p1_ref[at, :].astype(F32)
            out[z] = (total + p2_ref[at, :].astype(F32) + p3_ref[at, :].astype(F32)).astype(BF16)


def fold(core, parts):
    half = jax.ShapeDtypeStruct((NZ, 16, 512), BF16)
    return pl.pallas_call(
        fold_kernel,
        out_shape=(half, half),
        in_specs=[SM] + [VM] * 4,
        out_specs=(VM, VM),
        compiler_params=pltpu.CompilerParams(vmem_limit_bytes=4 << 20),
        cost_estimate=pl.CostEstimate(flops=1 << 18, bytes_accessed=1 << 19, transcendentals=0),
        name="fold",
    )(core, *parts)


def scatter(parts, core):
    line = total([parts[0], *shifted(1, parts[1:])])
    keep, send = fold(core, [line[0], *shifted(0, line[1:])])
    ring = small(join_kernel, "join", (NZ, NH, 16, 512), core, keep, swap(send))
    ring = lax.all_to_all(ring.reshape(NZ * NH, 16, 512), ("zl", "zh"), 0, 0)
    return jnp.sum(ring.astype(F32), axis=0)


def body(queries, memory, key_weight, value_weight, grad_context, memory_lengths):
    here = [lax.axis_index(name).astype(jnp.int32).reshape(1) for name in ("core", "y", "x")]
    core = here[0]
    blocks = gather(memory, core)
    key_weight, value_weight = stage(key_weight, value_weight, blocks[0])
    other = project(True, here, blocks, key_weight, value_weight)
    got = swap(other)
    own = project(False, here, blocks, key_weight, value_weight)
    ctx, gq, mine = attend(core, memory_lengths, own, got, queries, grad_context)
    parts = back(here, mine, swap(mine), key_weight, value_weight)
    return ctx, gq, scatter(parts, core)


def solution(mesh):
    fine = Mesh(mesh.devices.reshape(NZ, NY, NC, NH, NX), AXES)
    spec = P(("zl", "y", "core"), ("zh", "x"))
    return jax.shard_map(
        body,
        mesh=fine,
        in_specs=(spec, spec, spec, spec, spec, P()),
        out_specs=(spec, spec, spec),
        check_vma=False,
    )
```

```python
import functools

import jax
import jax.numpy as jnp
from jax import lax
from jax.experimental import pallas as pl
from jax.experimental.pallas import tpu as pltpu
from jax.sharding import Mesh, PartitionSpec as P

HDIM = 64
AXES = ("zl", "y", "core", "zh", "x")
NZ, NY, NC, NH, NX = 4, 4, 2, 2, 4
F32, BF16 = jnp.float32, jnp.bfloat16
VM = pl.BlockSpec(memory_space=pltpu.VMEM)
SM = pl.BlockSpec(memory_space=pltpu.SMEM)


def nt(a, b):
    return lax.dot_general(a, b, (((1,), (1,)), ((), ())), preferred_element_type=F32)


def nn(a, b):
    return lax.dot_general(a, b, (((1,), (0,)), ((), ())), preferred_element_type=F32)


def place(core, y, x, far, near):
    return jnp.where(core == 0, y + far, y + near) % NY, jnp.where(core == 0, x + near, x + far) % NX


def project_kernel(other, core_ref, y_ref, x_ref, b0_ref, b1_ref, b2_ref, b3_ref, wk_ref, wv_ref, out_ref, rows_ref):
    base = (1 - core_ref[0] if other else core_ref[0]) * 64
    for far, ref in enumerate((b0_ref, b1_ref, b2_ref, b3_ref)):
        for near in range(4):
            y, x = place(core_ref[0], y_ref[0], x_ref[0], 4 - far, 4 - near)
            for i in range(2):
                start = pl.multiple_of(base + 32 * i, 32)
                row = pl.multiple_of(128 * i + 32 * y, 32)
                rows_ref[x, pl.ds(row, 32), :] = ref[near, pl.ds(start, 32), :]
    rows = jnp.concatenate([rows_ref[x] for x in range(NX)], axis=1)
    out_ref[0] = nn(rows, wk_ref[...])
    out_ref[1] = nn(rows, wv_ref[...])


def project(other, here, blocks, wk, wv):
    return pl.pallas_call(
        functools.partial(project_kernel, other),
        out_shape=jax.ShapeDtypeStruct((2, 256, 512), F32),
        in_specs=[SM] * 3 + [VM] * 6,
        out_specs=VM,
        scratch_shapes=[pltpu.VMEM((NX, 256, 512), BF16)],
        compiler_params=pltpu.CompilerParams(vmem_limit_bytes=20 << 20),
        cost_estimate=pl.CostEstimate(flops=2 * 2 * 256 * 2048 * 512, bytes_accessed=7 << 20, transcendentals=0),
        name="project",
    )(*here, *blocks, wk, wv)


def split(a):
    low = lax.broadcasted_iota(jnp.int32, (128, 128), 1) < HDIM
    a, zero = a.astype(F32), jnp.zeros((128, 128), F32)
    return jnp.concatenate([jnp.where(low, a, zero), jnp.where(low, zero, a)], axis=0).astype(BF16)


def attend_kernel(pair_ref, len_ref, own_ref, got_ref, q_ref, g_ref, grad_ref, kv_ref, pb_ref, ds_ref):
    scale = HDIM ** (-0.5)
    token = lax.broadcasted_iota(jnp.int32, (2, 128, 128), 1)
    for i in range(2):
        valid = token < len_ref[pair_ref[0] * 2 + i]
        for p in range(4):
            at = (slice(128 * i, 128 * (i + 1)), slice(128 * p, 128 * (p + 1)))
            k = (own_ref[0][at] + got_ref[0][at]).astype(BF16)
            v = (own_ref[1][at] + got_ref[1][at]).astype(BF16)
            kv_ref[(0, *at)], kv_ref[(1, *at)] = k, v
            q, g = q_ref[at], g_ref[at]
            s = nt(split(k), q).reshape(2, 128, 128) * scale
            s = jnp.where(valid, s, F32(-1e30))
            e = jnp.exp(s - jnp.max(s, axis=1, keepdims=True))
            prob = e / jnp.sum(e, axis=1, keepdims=True)
            dp = nt(split(v), g).reshape(2, 128, 128)
            delta = jnp.sum(prob * dp, axis=1, keepdims=True)
            ds = (prob * (dp - delta) * scale).astype(BF16)
            pb = prob.astype(BF16)
            pb_ref[4 * i + p], ds_ref[4 * i + p] = pb.reshape(256, 128), ds.reshape(256, 128)
            grad_ref[(0, *at)] = nn(jnp.concatenate([ds[0], ds[1]], axis=1), split(q)).astype(BF16)
            grad_ref[(1, *at)] = nn(jnp.concatenate([pb[0], pb[1]], axis=1), split(g)).astype(BF16)


def attend(pair, lengths, own, got, q, g):
    two = jax.ShapeDtypeStruct((2, 256, 512), BF16)
    weights = jax.ShapeDtypeStruct((8, 256, 128), BF16)
    return pl.pallas_call(
        attend_kernel,
        out_shape=(two, two, weights, weights),
        in_specs=[SM, SM, VM, VM, VM, VM],
        out_specs=(VM,) * 4,
        compiler_params=pltpu.CompilerParams(vmem_limit_bytes=20 << 20),
        cost_estimate=pl.CostEstimate(flops=4 * 8 * 2 * 256 * 128 * 128, bytes_accessed=4 << 20, transcendentals=1 << 18),
        name="attend",
    )(pair, lengths, own, got, q, g)


def finish_kernel(kv_ref, pb_ref, ds_ref, ctx_ref, gq_ref, mark_ref):
    mark_ref[...] = jnp.zeros((8, 128), F32)
    for i in range(2):
        for p in range(4):
            at = (slice(128 * i, 128 * (i + 1)), slice(128 * p, 128 * (p + 1)))
            ctx_ref[at] = nn(pb_ref[4 * i + p].T, split(kv_ref[(1, *at)])).astype(BF16)
            gq_ref[at] = nn(ds_ref[4 * i + p].T, split(kv_ref[(0, *at)])).astype(BF16)


def finish(kv, pb, ds):
    one = jax.ShapeDtypeStruct((256, 512), BF16)
    return pl.pallas_call(
        finish_kernel,
        out_shape=(one, one, jax.ShapeDtypeStruct((8, 128), F32)),
        in_specs=[VM] * 3,
        out_specs=(VM, VM, VM),
        compiler_params=pltpu.CompilerParams(vmem_limit_bytes=12 << 20),
        cost_estimate=pl.CostEstimate(flops=2 * 8 * 2 * 256 * 128 * 128, bytes_accessed=2 << 20, transcendentals=0),
        name="finish",
    )(kv, pb, ds)


def stage_kernel(wk_ref, wv_ref, after_ref, k_ref, v_ref, sems):
    copies = [
        pltpu.make_async_copy(wk_ref, k_ref, sems.at[0]),
        pltpu.make_async_copy(wv_ref, v_ref, sems.at[1]),
    ]
    for copy in copies:
        copy.start()
    for copy in copies:
        copy.wait()


def stage(wk, wv, after):
    leave = pl.BlockSpec(memory_space=pl.ANY)
    return pl.pallas_call(
        stage_kernel,
        out_shape=(jax.ShapeDtypeStruct(wk.shape, BF16), jax.ShapeDtypeStruct(wv.shape, BF16)),
        in_specs=[leave, leave, leave],
        out_specs=(VM, VM),
        scratch_shapes=[pltpu.SemaphoreType.DMA((2,))],
        compiler_params=pltpu.CompilerParams(vmem_limit_bytes=10 << 20),
        cost_estimate=pl.CostEstimate(flops=0, bytes_accessed=8 << 20, transcendentals=0),
        name="stage",
    )(wk, wv, after)


def back_kernel(core_ref, y_ref, x_ref, grad_ref, wk_ref, wv_ref, o0_ref, o1_ref, o2_ref, o3_ref, all_ref):
    for x in range(NX):
        at = slice(512 * x, 512 * (x + 1))
        r = (nt(grad_ref[0], wk_ref[at]) + nt(grad_ref[1], wv_ref[at])).astype(BF16)
        for i in range(2):
            all_ref[:, x, 32 * i : 32 * (i + 1), :] = r[128 * i : 128 * (i + 1)].reshape(NY, 32, 512)
    for far, ref in enumerate((o0_ref, o1_ref, o2_ref, o3_ref)):
        for near in range(4):
            y, x = place(core_ref[0], y_ref[0], x_ref[0], far, near)
            ref[near] = all_ref[y, x]


def back(here, grads, wk, wv):
    part = jax.ShapeDtypeStruct((4, 64, 512), BF16)
    return pl.pallas_call(
        back_kernel,
        out_shape=(part,) * 4,
        in_specs=[SM] * 3 + [VM] * 3,
        out_specs=(VM,) * 4,
        scratch_shapes=[pltpu.VMEM((NY, NX, 64, 512), BF16)],
        compiler_params=pltpu.CompilerParams(vmem_limit_bytes=20 << 20),
        cost_estimate=pl.CostEstimate(flops=2 * 2 * 256 * 2048 * 512, bytes_accessed=6 << 20, transcendentals=0),
        name="back",
    )(*here, grads, wk, wv)


def swap(block):
    return lax.ppermute(block, "core", [(0, 1), (1, 0)])


def route(along, shift):
    pairs = []
    for y in range(NY):
        for c in range(NC):
            for x in range(NX):
                to = (y, (x + shift) % NX) if c == along else ((y + shift) % NY, x)
                pairs.append(((y * NC + c) * NX + x, (to[0] * NC + c) * NX + to[1]))
    return pairs


def shifted(along, blocks):
    return [lax.ppermute(b, ("y", "core", "x"), route(along, k)) for k, b in zip((1, 2, 3), blocks)]


def column_kernel(core_ref, ring_ref, got_ref, out_ref):
    core = core_ref[0]
    for z in range(NZ):
        own = pl.multiple_of(32 * z + 16 * core, 16)
        out_ref[pl.ds(own, 16), :] = ring_ref[z, core]
        other = pl.multiple_of(32 * z + 16 * (1 - core), 16)
        out_ref[pl.ds(other, 16), :] = got_ref[z]


def pack_kernel(core_ref, *refs):
    for k in range(4):
        refs[4][k] = refs[k][...]


def spread_kernel(core_ref, block_ref, out_ref):
    block = block_ref[...]
    for k in range(NZ * NH):
        out_ref[k] = block


def pick_kernel(core_ref, ring_ref, out_ref):
    for z in range(NZ):
        out_ref[z] = ring_ref[z, 1 - core_ref[0]]


def join_kernel(core_ref, keep_ref, got_ref, out_ref):
    for z in range(NZ):
        out_ref[z, core_ref[0]] = keep_ref[z]
        out_ref[z, 1 - core_ref[0]] = got_ref[z]


def small(kernel, name, shape, *args):
    return pl.pallas_call(
        kernel,
        out_shape=jax.ShapeDtypeStruct(shape, BF16),
        in_specs=[SM] + [VM] * (len(args) - 1),
        out_specs=VM,
        compiler_params=pltpu.CompilerParams(vmem_limit_bytes=4 << 20),
        cost_estimate=pl.CostEstimate(flops=0, bytes_accessed=1 << 18, transcendentals=0),
        name=name,
    )(*args)


def gather(memory, core):
    copies = small(spread_kernel, "spread", (NZ * NH, 16, 512), core, memory)
    ring = lax.all_to_all(copies, ("zl", "zh"), 0, 0).reshape(NZ, NH, 16, 512)
    got = swap(small(pick_kernel, "pick", (NZ, 16, 512), core, ring))
    column = small(column_kernel, "column", (128, 512), core, ring, got)
    blocks = small(pack_kernel, "pack", (4, 128, 512), core, column, *shifted(0, [column] * 3))
    return [blocks, *shifted(1, [blocks] * 3)]


def total_kernel(core_ref, after_ref, *refs):
    for side in range(2):
        base = 64 * (core_ref[0] if side == 0 else 1 - core_ref[0])
        p0_ref, p1_ref, p2_ref, p3_ref = refs[4 * side : 4 * side + 4]
        for near in range(4):
            total = p0_ref[near].astype(F32) + p1_ref[near].astype(F32)
            total = (total + p2_ref[near].astype(F32) + p3_ref[near].astype(F32)).astype(BF16)
            refs[8 + near][pl.ds(pl.multiple_of(base, 64), 64), :] = total


def total(core, after, mine, theirs):
    one = jax.ShapeDtypeStruct((128, 512), BF16)
    return pl.pallas_call(
        total_kernel,
        out_shape=(one, one, one, one),
        in_specs=[SM] + [VM] * 9,
        out_specs=(VM,) * 4,
        compiler_params=pltpu.CompilerParams(vmem_limit_bytes=8 << 20),
        cost_estimate=pl.CostEstimate(flops=1 << 20, bytes_accessed=5 << 19, transcendentals=0),
        name="total",
    )(core, after, *mine, *theirs)


def fold_kernel(core_ref, p0_ref, p1_ref, p2_ref, p3_ref, keep_ref, send_ref):
    core = core_ref[0]
    for side, out in enumerate((keep_ref, send_ref)):
        half = core if side == 0 else 1 - core
        for z in range(NZ):
            at = pl.ds(pl.multiple_of(32 * z + 16 * half, 16), 16)
            total = p0_ref[at, :].astype(F32) + p1_ref[at, :].astype(F32)
            out[z] = (total + p2_ref[at, :].astype(F32) + p3_ref[at, :].astype(F32)).astype(BF16)


def fold(core, parts):
    half = jax.ShapeDtypeStruct((NZ, 16, 512), BF16)
    return pl.pallas_call(
        fold_kernel,
        out_shape=(half, half),
        in_specs=[SM] + [VM] * 4,
        out_specs=(VM, VM),
        compiler_params=pltpu.CompilerParams(vmem_limit_bytes=4 << 20),
        cost_estimate=pl.CostEstimate(flops=1 << 18, bytes_accessed=1 << 19, transcendentals=0),
        name="fold",
    )(core, *parts)


def scatter(mine, theirs, core, after):
    line = total(core, after, mine, theirs)
    keep, send = fold(core, [line[0], *shifted(0, line[1:])])
    ring = small(join_kernel, "join", (NZ, NH, 16, 512), core, keep, swap(send))
    ring = lax.all_to_all(ring.reshape(NZ * NH, 16, 512), ("zl", "zh"), 0, 0)
    return jnp.sum(ring.astype(F32), axis=0)


def body(queries, memory, key_weight, value_weight, grad_context, memory_lengths):
    here = [lax.axis_index(name).astype(jnp.int32).reshape(1) for name in ("core", "y", "x")]
    core = here[0]
    blocks = gather(memory, core)
    key_weight, value_weight = stage(key_weight, value_weight, blocks[0])
    got = swap(project(True, here, blocks, key_weight, value_weight))
    own = project(False, here, blocks, key_weight, value_weight)
    grads, kv, pb, ds = attend(core, memory_lengths, own, got, queries, grad_context)
    mine = back(here, grads, key_weight, value_weight)
    mine = [mine[0], *shifted(1, mine[1:])]
    theirs = back(here, swap(grads), key_weight, value_weight)
    theirs = [theirs[0], *shifted(1, theirs[1:])]
    ctx, gq, mark = finish(kv, pb, ds)
    return ctx, gq, scatter(mine, theirs, core, mark)


def solution(mesh):
    fine = Mesh(mesh.devices.reshape(NZ, NY, NC, NH, NX), AXES)
    spec = P(("zl", "y", "core"), ("zh", "x"))
    return jax.shard_map(
        body,
        mesh=fine,
        in_specs=(spec, spec, spec, spec, spec, P()),
        out_specs=(spec, spec, spec),
        check_vma=False,
    )
```
